32 devices in a mesh: win: 4 (over z), sec: 8 (over y, x, core).
Axes of the slice: x: 2, y: 2, z: 4, core: 2. Of those that a mesh axis runs over, the one named last changes fastest.
Arguments:
- initial: bfloat16 [5, 8, 24, 512], P(None, 'win'), may hold values from -6 to 6
- props: bfloat16 [8, 8, 2, 256, 256], P('sec'), may hold values from -0.25 to 0.25
- screen: float32 [8, 8, 256], P('sec', 'win'), may hold values from -3.140625 to 3.140625
- links: int32 [8, 8, 6], P('sec', 'win'), may hold values from 0 to 7, as said below
- kinds: int32 [8, 8, 6], P('sec', 'win'), may hold values from 0 to 7
- counts: int32 [8, 8], P('sec', 'win'), may hold values from 1 to 6
Outputs:
- fields: bfloat16 [8, 5, 8, 24, 512], P('sec', None, 'win')
The draws below stay inside these ranges and needn't reach their ends.
Inputs may be any that keep to these rules, and one draw needn't show every extreme that they name: links[s, w, l] lies within w - 1 to w + 1.
All inputs are finite; a program needn't handle non-finite values.
Results may differ from the reference program's by a relative error of at most 0.033.
Values may be sent and summed in bfloat16 or wider, within the bound.
A program may use at most 64 MiB of HBM per device.

```python
import jax
import jax.numpy as jnp
from jax import lax

K = 256
S = 24
F = 5
L = 6
NPROP = 8
W = 8
NSEC = 8


def draw_links(key, part):
    offsets = jax.random.randint(key, (NSEC, W, L), -1, 2)
    base = jnp.arange(W, dtype=jnp.int32)[None, :, None]
    return jnp.clip(base + offsets, 0, W - 1).astype(jnp.int32)


def with_ends(entries, key, least, largest):
    longest = entries.shape.index(max(entries.shape))
    spots = []
    for shift in (0, 1):
        where = [jax.random.randint(jax.random.fold_in(key, axis), (), 0, length) for axis, length in enumerate(entries.shape)]
        where[longest] = (where[longest] + shift) % entries.shape[longest]
        spots.append(tuple(where))
    return entries.at[spots[0]].set(least).at[spots[1]].set(largest)


def block_levels(rng, shape, pieces, low, high):
    level = 1.0
    for axis_at, blocks in pieces:
        steps = jax.random.uniform(jax.random.fold_in(jax.random.fold_in(rng, 6), axis_at), (blocks,), jnp.float32, low / len(pieces), high / len(pieces))
        level = level * jnp.repeat(jnp.exp(steps), shape[axis_at] // blocks).reshape((-1,) + (1,) * (len(shape) - 1 - axis_at))
    return level


def gaussian(own_key, shape, scale, limit, cuts=(), kind=jnp.bfloat16):
    entries = scale * jax.random.normal(own_key, shape, jnp.float32)
    if cuts:
        entries = entries * block_levels(own_key, shape, cuts, -0.22, 0.18)
    return jnp.clip(entries, -limit, limit).astype(kind)


def setup_inputs(seed: int = 0) -> dict:
    splits = jax.random.split(jax.random.key(seed), 7)
    return {
        "initial": gaussian(splits[0], (F, W, S, 2 * K), 1.0, 6.0, ((1, 4),)),
        "props": gaussian(splits[1], (NSEC, NPROP, 2, K, K), (2 * K) ** -0.5, 0.25, ((0, 8),)),
        "screen": jnp.clip(jax.random.uniform(splits[2], (NSEC, W, K), jnp.float32, -3.140625, 3.140625), -3.140625, 3.140625),
        "links": draw_links(jax.random.fold_in(splits[6], 71), 0),
        "kinds": with_ends(jax.random.randint(splits[4], (NSEC, W, L), 0, NPROP), jax.random.fold_in(splits[4], 1), 0, NPROP - 1).astype(jnp.int32),
        "counts": with_ends(jax.random.randint(splits[5], (NSEC, W), 1, L + 1), jax.random.fold_in(splits[5], 1), 1, L).astype(jnp.int32),
    }


def build_blocks(section_table):
    real_part = section_table[:, 0].astype(jnp.float32)
    imag_part = section_table[:, 1].astype(jnp.float32)
    upper = jnp.concatenate([real_part, imag_part], axis=-1)
    lower = jnp.concatenate([-imag_part, real_part], axis=-1)
    return jnp.concatenate([upper, lower], axis=-2)

def section_step(field, inputs):
    section_table, screen_phase, link_rows, kind_rows, count_rows = inputs
    blocks = build_blocks(section_table)
    field_wide = field.astype(jnp.float32)
    gathered = field_wide[:, link_rows]
    scaled = lax.rsqrt(count_rows.astype(jnp.float32))
    weighting = (jnp.arange(L)[None, :] < count_rows[:, None]).astype(jnp.float32) * scaled[:, None]
    total = jnp.zeros(field.shape, jnp.float32)
    for entry in range(NPROP):
        picked = weighting * (kind_rows == entry).astype(jnp.float32)
        mixed = jnp.einsum('wl,fwlsc->fwsc', picked, gathered, precision=lax.Precision.HIGHEST)
        total = total + jnp.einsum('fwsc,cd->fwsd', mixed, blocks[entry], precision=lax.Precision.HIGHEST)
    real_out = total[..., :K]
    imag_out = total[..., K:]
    cosine = jnp.cos(screen_phase)[None, :, None, :]
    sine_part = jnp.sin(screen_phase)[None, :, None, :]
    result = jnp.concatenate([real_out * cosine - imag_out * sine_part, real_out * sine_part + imag_out * cosine], axis=-1).astype(jnp.bfloat16)
    return (result, result)

def reference(initial, props, screen, links, kinds, counts):
    final_field, fields = lax.scan(section_step, initial, (props, screen, links, kinds, counts))
    return fields
```

```python
import functools

import jax
import jax.numpy as jnp
from jax import lax
from jax.experimental import pallas as pl
from jax.experimental.pallas import tpu as pltpu
from jax.sharding import PartitionSpec as P

MESH = pl.DeviceIdType.MESH


def kernel(
    wins, secs, links, kinds, counts, screen, initial, props, out,
    inbox, table, mixed, coef, turn, table_sem, seed_sem, send_sem, recv_sem,
):
    z = lax.axis_index("win")
    s = lax.axis_index("sec")
    fronts, local, sources, width = initial.shape
    coeffs = width // 2
    entries = props.shape[0] // width
    length = links.shape[2]
    has_low = z > 0
    has_high = z < wins - 1
    first = s == 0
    sends = s < secs - 1

    load_table = pltpu.make_async_copy(props, table, table_sem)
    load_table.start()

    barrier = pltpu.get_barrier_semaphore()

    def greet(win, sec):
        pl.semaphore_signal(barrier, inc=1, device_id=(win, sec), device_id_type=MESH)

    @pl.when(s > 0)
    def _():
        greet(z, s - 1)

    @pl.when(has_low)
    def _():
        greet(z - 1, jnp.maximum(s - 1, 0))

    @pl.when(has_high)
    def _():
        greet(z + 1, jnp.maximum(s - 1, 0))

    sides = has_low.astype(jnp.int32) + has_high.astype(jnp.int32)
    expected = jnp.where(sends, 1 + sides, 0) + jnp.where(first, sides, 0)

    @pl.when(expected > 0)
    def _():
        pl.semaphore_wait(barrier, expected)

    def remote(source, target, send, receive, win, sec):
        return pltpu.make_async_remote_copy(
            src_ref=source, dst_ref=target, send_sem=send, recv_sem=receive,
            device_id=(win, sec), device_id_type=MESH,
        )

    def seed_own(f):
        return pltpu.make_async_copy(
            initial.at[f], inbox.at[f, pl.ds(1, local)], recv_sem.at[f, 0]
        )

    def seed_low(f):
        return remote(
            initial.at[f, 0], inbox.at[f, local + 1], seed_sem.at[f, 0], recv_sem.at[f, 2], z - 1, s
        )

    def seed_high(f):
        return remote(
            initial.at[f, local - 1], inbox.at[f, 0], seed_sem.at[f, 1], recv_sem.at[f, 1], z + 1, s
        )

    @pl.when(first & has_low)
    def _():
        for f in range(fronts):
            seed_low(f).start()

    @pl.when(first & has_high)
    def _():
        for f in range(fronts):
            seed_high(f).start()

    @pl.when(first)
    def _():
        for f in range(fronts):
            seed_own(f).start()

    @pl.when(jnp.logical_not(has_low))
    def _():
        inbox[:, 0] = jnp.zeros((fronts, sources, width), jnp.bfloat16)

    @pl.when(jnp.logical_not(has_high))
    def _():
        inbox[:, local + 1] = jnp.zeros((fronts, sources, width), jnp.bfloat16)

    for w in range(local):
        live = counts[0, w]
        codes = []
        for l in range(length):
            offset = links[0, w, l] - (z * local + w - 1)
            codes.append(jnp.where(l < live, kinds[0, w, l] * 3 + offset, -1))
        for code in range(entries * 3):
            hits = sum((c == code).astype(jnp.int32) for c in codes)
            coef[w, code] = hits.astype(jnp.float32)
        scale = lax.rsqrt(jnp.full((1, coeffs), live, jnp.int32).astype(jnp.float32))
        phase = screen[0, pl.ds(w, 1), :]
        turn[w, 0] = jnp.broadcast_to(jnp.cos(phase) * scale, turn.shape[2:])
        turn[w, 1] = jnp.broadcast_to(jnp.sin(phase) * scale, turn.shape[2:])

    load_table.wait()

    def send_own(f):
        return remote(
            out.at[0, f], inbox.at[f, pl.ds(1, local)], send_sem.at[f, 0], recv_sem.at[f, 0], z, s + 1
        )

    def send_low(f):
        return remote(
            out.at[0, f, 0], inbox.at[f, local + 1], send_sem.at[f, 1], recv_sem.at[f, 2], z - 1, s + 1
        )

    def send_high(f):
        return remote(
            out.at[0, f, local - 1], inbox.at[f, 0], send_sem.at[f, 2], recv_sem.at[f, 1], z + 1, s + 1
        )

    def arrived(ref, sem):
        pltpu.make_async_copy(ref, ref, sem).wait()

    half = entries * width // 2

    def step(f, carry):
        arrived(inbox.at[f, pl.ds(1, local)], recv_sem.at[f, 0])

        @pl.when(has_low)
        def _():
            arrived(inbox.at[f, 0], recv_sem.at[f, 1])

        @pl.when(has_high)
        def _():
            arrived(inbox.at[f, local + 1], recv_sem.at[f, 2])

        held = [inbox[f, j].astype(jnp.float32) for j in range(local + 2)]
        for entry in range(entries):
            straight, crossed = [], []
            for w in range(local):
                total = coef[w, entry * 3] * held[w]
                for d in (1, 2):
                    total = total + coef[w, entry * 3 + d] * held[w + d]
                a, b = total[:, :coeffs], total[:, coeffs:]
                straight += [a, b]
                crossed += [-b, a]
            left = entry * width
            mixed[:, left : left + coeffs] = jnp.concatenate(straight, 0).astype(jnp.bfloat16)
            mixed[:, left + coeffs : left + width] = jnp.concatenate(crossed, 0).astype(jnp.bfloat16)
        total = jnp.dot(
            mixed[:, :half], table[:half], preferred_element_type=jnp.float32
        ) + jnp.dot(mixed[:, half:], table[half:], preferred_element_type=jnp.float32)
        for w in range(local):
            top = 2 * w * sources
            a = total[top : top + sources]
            b = total[top + sources : top + 2 * sources]
            c = turn[w, 0, :1]
            d = turn[w, 1, :1]
            out[0, f, w, :, :coeffs] = (a * c - b * d).astype(jnp.bfloat16)
            out[0, f, w, :, coeffs:] = (a * d + b * c).astype(jnp.bfloat16)

        @pl.when(sends & has_low)
        def _():
            send_low(f).start()

        @pl.when(sends & has_high)
        def _():
            send_high(f).start()

        @pl.when(sends)
        def _():
            send_own(f).start()

        return carry

    lax.fori_loop(0, fronts, step, 0)

    @pl.when(first & has_low)
    def _():
        for f in range(fronts):
            seed_low(f).wait_send()

    @pl.when(first & has_high)
    def _():
        for f in range(fronts):
            seed_high(f).wait_send()

    @pl.when(sends & has_low)
    def _():
        for f in range(fronts):
            send_low(f).wait_send()

    @pl.when(sends & has_high)
    def _():
        for f in range(fronts):
            send_high(f).wait_send()

    @pl.when(sends)
    def _():
        for f in range(fronts):
            send_own(f).wait_send()


def solution(mesh):
    wins, secs = mesh.shape["win"], mesh.shape["sec"]

    def run(initial, props, screen, links, kinds, counts):
        fronts, local, sources, width = initial.shape
        coeffs = width // 2
        entries = props.shape[1]
        smem = pl.BlockSpec(memory_space=pltpu.SMEM)
        vmem = pl.BlockSpec(memory_space=pltpu.VMEM)
        whole = pl.BlockSpec(memory_space=pl.ANY)
        return pl.pallas_call(
            functools.partial(kernel, wins, secs),
            out_shape=jax.ShapeDtypeStruct((1, fronts, local, sources, width), jnp.bfloat16),
            in_specs=[smem, smem, smem, vmem, whole, whole],
            out_specs=vmem,
            scratch_shapes=[
                pltpu.VMEM((fronts, local + 2, sources, width), jnp.bfloat16),
                pltpu.VMEM((entries * width, coeffs), jnp.bfloat16),
                pltpu.VMEM((2 * local * sources, entries * width), jnp.bfloat16),
                pltpu.SMEM((local, 3 * entries), jnp.float32),
                pltpu.VMEM((local, 2, 8, coeffs), jnp.float32),
                pltpu.SemaphoreType.DMA,
                pltpu.SemaphoreType.DMA((fronts, 2)),
                pltpu.SemaphoreType.DMA((fronts, 3)),
                pltpu.SemaphoreType.DMA((fronts, 3)),
            ],
            compiler_params=pltpu.CompilerParams(collective_id=0, has_side_effects=True),
            name="beamlets",
        )(links, kinds, counts, screen, initial, props.reshape(entries * width, coeffs))

    placed = (
        P(None, "win", None, None),
        P("sec", None, None, None, None),
        P("sec", "win", None),
        P("sec", "win", None),
        P("sec", "win", None),
        P("sec", "win"),
    )
    return jax.shard_map(
        run,
        mesh=mesh,
        in_specs=placed,
        out_specs=P("sec", None, "win", None, None),
        check_vma=False,
    )
```

```python
import functools

import jax
import jax.numpy as jnp
from jax import lax
from jax.experimental import pallas as pl
from jax.experimental.pallas import tpu as pltpu
from jax.sharding import PartitionSpec as P

MESH = pl.DeviceIdType.MESH


def kernel(
    wins, secs, links, kinds, counts, screen, initial, props, out,
    inbox, table, mixed, coef, turn, table_sem, seed_sem, send_sem, recv_sem,
):
    z = lax.axis_index("win")
    s = lax.axis_index("sec")
    fronts, local, sources, width = initial.shape
    coeffs = width // 2
    entries = props.shape[0]
    length = links.shape[2]
    has_low = z > 0
    has_high = z < wins - 1
    first = s == 0
    sends = s < secs - 1

    loads = [
        pltpu.make_async_copy(props.at[:, part], table.at[part], table_sem.at[part])
        for part in (0, 1)
    ]
    for load in loads:
        load.start()

    barrier = pltpu.get_barrier_semaphore()

    def greet(win, sec):
        pl.semaphore_signal(barrier, inc=1, device_id=(win, sec), device_id_type=MESH)

    @pl.when(s > 0)
    def _():
        greet(z, s - 1)

    @pl.when(has_low)
    def _():
        greet(z - 1, jnp.maximum(s - 1, 0))

    @pl.when(has_high)
    def _():
        greet(z + 1, jnp.maximum(s - 1, 0))

    sides = has_low.astype(jnp.int32) + has_high.astype(jnp.int32)
    expected = jnp.where(sends, 1 + sides, 0) + jnp.where(first, sides, 0)

    @pl.when(expected > 0)
    def _():
        pl.semaphore_wait(barrier, expected)

    def remote(source, target, send, receive, win, sec):
        return pltpu.make_async_remote_copy(
            src_ref=source, dst_ref=target, send_sem=send, recv_sem=receive,
            device_id=(win, sec), device_id_type=MESH,
        )

    def seed_own(f):
        return pltpu.make_async_copy(
            initial.at[f], inbox.at[f, pl.ds(1, local)], recv_sem.at[f, 0]
        )

    def seed_low(f):
        return remote(
            initial.at[f, 0], inbox.at[f, local + 1], seed_sem.at[f, 0], recv_sem.at[f, 2], z - 1, s
        )

    def seed_high(f):
        return remote(
            initial.at[f, local - 1], inbox.at[f, 0], seed_sem.at[f, 1], recv_sem.at[f, 1], z + 1, s
        )

    @pl.when(first & has_low)
    def _():
        for f in range(fronts):
            seed_low(f).start()

    @pl.when(first & has_high)
    def _():
        for f in range(fronts):
            seed_high(f).start()

    @pl.when(first)
    def _():
        for f in range(fronts):
            seed_own(f).start()

    @pl.when(jnp.logical_not(has_low))
    def _():
        inbox[:, 0] = jnp.zeros((fronts, sources, width), jnp.bfloat16)

    @pl.when(jnp.logical_not(has_high))
    def _():
        inbox[:, local + 1] = jnp.zeros((fronts, sources, width), jnp.bfloat16)

    for w in range(local):
        live = counts[0, w]
        codes = []
        for l in range(length):
            offset = links[0, w, l] - (z * local + w - 1)
            codes.append(jnp.where(l < live, kinds[0, w, l] * 3 + offset, -1))
        for code in range(entries * 3):
            hits = sum((c == code).astype(jnp.int32) for c in codes)
            coef[w, code] = hits.astype(jnp.float32)
        scale = lax.rsqrt(jnp.full((1, coeffs), live, jnp.int32).astype(jnp.float32))
        phase = screen[0, pl.ds(w, 1), :]
        turn[w, 0] = jnp.broadcast_to(jnp.cos(phase) * scale, turn.shape[2:])
        turn[w, 1] = jnp.broadcast_to(jnp.sin(phase) * scale, turn.shape[2:])

    for load in loads:
        load.wait()

    def send_own(f):
        return remote(
            out.at[0, f], inbox.at[f, pl.ds(1, local)], send_sem.at[f, 0], recv_sem.at[f, 0], z, s + 1
        )

    def send_low(f):
        return remote(
            out.at[0, f, 0], inbox.at[f, local + 1], send_sem.at[f, 1], recv_sem.at[f, 2], z - 1, s + 1
        )

    def send_high(f):
        return remote(
            out.at[0, f, local - 1], inbox.at[f, 0], send_sem.at[f, 2], recv_sem.at[f, 1], z + 1, s + 1
        )

    def arrived(ref, sem):
        pltpu.make_async_copy(ref, ref, sem).wait()

    depth = entries * coeffs

    def step(f, carry):
        arrived(inbox.at[f, pl.ds(1, local)], recv_sem.at[f, 0])

        @pl.when(has_low)
        def _():
            arrived(inbox.at[f, 0], recv_sem.at[f, 1])

        @pl.when(has_high)
        def _():
            arrived(inbox.at[f, local + 1], recv_sem.at[f, 2])

        held = [inbox[f, j].astype(jnp.float32) for j in range(local + 2)]
        for entry in range(entries):
            stack = []
            for w in range(local):
                total = coef[w, entry * 3] * held[w]
                for d in (1, 2):
                    total = total + coef[w, entry * 3 + d] * held[w + d]
                a, b = total[:, :coeffs], total[:, coeffs:]
                stack += [a, b]
            left = entry * coeffs
            mixed[:, left : left + coeffs] = jnp.concatenate(stack, 0).astype(jnp.bfloat16)
        lhs = mixed[...]
        by_real, by_imag = (
            jnp.dot(lhs, table[part].reshape(depth, coeffs), preferred_element_type=jnp.float32)
            for part in (0, 1)
        )
        for w in range(local):
            top = 2 * w * sources
            mid, low = top + sources, top + 2 * sources
            a = by_real[top:mid] - by_imag[mid:low]
            b = by_real[mid:low] + by_imag[top:mid]
            c = turn[w, 0, :1]
            d = turn[w, 1, :1]
            out[0, f, w, :, :coeffs] = (a * c - b * d).astype(jnp.bfloat16)
            out[0, f, w, :, coeffs:] = (a * d + b * c).astype(jnp.bfloat16)

        @pl.when(f >= 2)
        def _():
            @pl.when(sends & has_low)
            def _():
                send_low(f - 2).wait_send()

            @pl.when(sends & has_high)
            def _():
                send_high(f - 2).wait_send()

            @pl.when(sends)
            def _():
                send_own(f - 2).wait_send()

        @pl.when(sends & has_low)
        def _():
            send_low(f).start()

        @pl.when(sends & has_high)
        def _():
            send_high(f).start()

        @pl.when(sends)
        def _():
            send_own(f).start()

        return carry

    lax.fori_loop(0, fronts, step, 0)

    @pl.when(first & has_low)
    def _():
        for f in range(fronts):
            seed_low(f).wait_send()

    @pl.when(first & has_high)
    def _():
        for f in range(fronts):
            seed_high(f).wait_send()

    @pl.when(sends & has_low)
    def _():
        for f in range(max(fronts - 2, 0), fronts):
            send_low(f).wait_send()

    @pl.when(sends & has_high)
    def _():
        for f in range(max(fronts - 2, 0), fronts):
            send_high(f).wait_send()

    @pl.when(sends)
    def _():
        for f in range(max(fronts - 2, 0), fronts):
            send_own(f).wait_send()


def solution(mesh):
    wins, secs = mesh.shape["win"], mesh.shape["sec"]

    def run(initial, props, screen, links, kinds, counts):
        fronts, local, sources, width = initial.shape
        coeffs = width // 2
        entries = props.shape[1]
        smem = pl.BlockSpec(memory_space=pltpu.SMEM)
        vmem = pl.BlockSpec(memory_space=pltpu.VMEM)
        whole = pl.BlockSpec(memory_space=pl.ANY)
        return pl.pallas_call(
            functools.partial(kernel, wins, secs),
            out_shape=jax.ShapeDtypeStruct((1, fronts, local, sources, width), jnp.bfloat16),
            in_specs=[smem, smem, smem, vmem, whole, whole],
            out_specs=vmem,
            scratch_shapes=[
                pltpu.VMEM((fronts, local + 2, sources, width), jnp.bfloat16),
                pltpu.VMEM((2, entries, coeffs, coeffs), jnp.bfloat16),
                pltpu.VMEM((2 * local * sources, entries * coeffs), jnp.bfloat16),
                pltpu.SMEM((local, 3 * entries), jnp.float32),
                pltpu.VMEM((local, 2, 8, coeffs), jnp.float32),
                pltpu.SemaphoreType.DMA((2,)),
                pltpu.SemaphoreType.DMA((fronts, 2)),
                pltpu.SemaphoreType.DMA((fronts, 3)),
                pltpu.SemaphoreType.DMA((fronts, 3)),
            ],
            compiler_params=pltpu.CompilerParams(collective_id=0, has_side_effects=True),
            name="beamlets",
        )(links, kinds, counts, screen, initial, props[0])

    placed = (
        P(None, "win", None, None),
        P("sec", None, None, None, None),
        P("sec", "win", None),
        P("sec", "win", None),
        P("sec", "win", None),
        P("sec", "win"),
    )
    return jax.shard_map(
        run,
        mesh=mesh,
        in_specs=placed,
        out_specs=P("sec", None, "win", None, None),
        check_vma=False,
    )
```

```python
import functools

import jax
import jax.numpy as jnp
from jax import lax
from jax.experimental import pallas as pl
from jax.experimental.pallas import tpu as pltpu
from jax.sharding import PartitionSpec as P

MESH = pl.DeviceIdType.MESH


def kernel(
    wins, secs, links, kinds, counts, screen, initial, props, out,
    inbox, table, mixed, coef, turn, table_sem, seed_sem, send_sem, recv_sem,
):
    z = lax.axis_index("win")
    s = lax.axis_index("sec")
    fronts, local, sources, width = initial.shape
    coeffs = width // 2
    entries = props.shape[0]
    length = links.shape[2]
    has_low = z > 0
    has_high = z < wins - 1
    first = s == 0
    sends = s < secs - 1

    loads = [
        pltpu.make_async_copy(props.at[:, part], table.at[part], table_sem.at[part])
        for part in (0, 1)
    ]
    for load in loads:
        load.start()

    barrier = pltpu.get_barrier_semaphore()

    def greet(win, sec):
        pl.semaphore_signal(barrier, inc=1, device_id=(win, sec), device_id_type=MESH)

    @pl.when(s > 0)
    def _():
        greet(z, s - 1)

    @pl.when(has_low)
    def _():
        greet(z - 1, jnp.maximum(s - 1, 0))

    @pl.when(has_high)
    def _():
        greet(z + 1, jnp.maximum(s - 1, 0))

    sides = has_low.astype(jnp.int32) + has_high.astype(jnp.int32)
    expected = jnp.where(sends, 1 + sides, 0) + jnp.where(first, sides, 0)

    @pl.when(expected > 0)
    def _():
        pl.semaphore_wait(barrier, expected)

    def remote(source, target, send, receive, win, sec):
        return pltpu.make_async_remote_copy(
            src_ref=source, dst_ref=target, send_sem=send, recv_sem=receive,
            device_id=(win, sec), device_id_type=MESH,
        )

    def seed_own(f):
        return pltpu.make_async_copy(
            initial.at[f], inbox.at[f, pl.ds(1, local)], recv_sem.at[f, 0]
        )

    def seed_low(f):
        return remote(
            initial.at[f, 0], inbox.at[f, local + 1], seed_sem.at[f, 0], recv_sem.at[f, 2], z - 1, s
        )

    def seed_high(f):
        return remote(
            initial.at[f, local - 1], inbox.at[f, 0], seed_sem.at[f, 1], recv_sem.at[f, 1], z + 1, s
        )

    @pl.when(first & has_low)
    def _():
        for f in range(fronts):
            seed_low(f).start()

    @pl.when(first & has_high)
    def _():
        for f in range(fronts):
            seed_high(f).start()

    @pl.when(first)
    def _():
        for f in range(fronts):
            seed_own(f).start()

    @pl.when(jnp.logical_not(has_low))
    def _():
        inbox[:, 0] = jnp.zeros((fronts, sources, width), jnp.bfloat16)

    @pl.when(jnp.logical_not(has_high))
    def _():
        inbox[:, local + 1] = jnp.zeros((fronts, sources, width), jnp.bfloat16)

    for w in range(local):
        live = counts[0, w]
        codes = []
        for l in range(length):
            offset = links[0, w, l] - (z * local + w - 1)
            codes.append(jnp.where(l < live, kinds[0, w, l] * 3 + offset, -1))
        for code in range(entries * 3):
            hits = sum((c == code).astype(jnp.int32) for c in codes)
            coef[w, code] = hits.astype(jnp.float32)
        scale = lax.rsqrt(jnp.full((1, coeffs), live, jnp.int32).astype(jnp.float32))
        phase = screen[0, pl.ds(w, 1), :]
        turn[w, 0] = jnp.broadcast_to(jnp.cos(phase) * scale, turn.shape[2:])
        turn[w, 1] = jnp.broadcast_to(jnp.sin(phase) * scale, turn.shape[2:])

    for load in loads:
        load.wait()

    def send_own(f):
        return remote(
            out.at[0, f], inbox.at[f, pl.ds(1, local)], send_sem.at[f, 0], recv_sem.at[f, 0], z, s + 1
        )

    def send_low(f):
        return remote(
            out.at[0, f, 0], inbox.at[f, local + 1], send_sem.at[f, 1], recv_sem.at[f, 2], z - 1, s + 1
        )

    def send_high(f):
        return remote(
            out.at[0, f, local - 1], inbox.at[f, 0], send_sem.at[f, 2], recv_sem.at[f, 1], z + 1, s + 1
        )

    def arrived(ref, sem):
        pltpu.make_async_copy(ref, ref, sem).wait()

    depth = entries * coeffs

    def step(f, carry):
        arrived(inbox.at[f, pl.ds(1, local)], recv_sem.at[f, 0])

        @pl.when(has_low)
        def _():
            arrived(inbox.at[f, 0], recv_sem.at[f, 1])

        @pl.when(has_high)
        def _():
            arrived(inbox.at[f, local + 1], recv_sem.at[f, 2])

        held = [inbox[f, j].astype(jnp.float32) for j in range(local + 2)]
        for entry in range(entries):
            stack = []
            for w in range(local):
                total = coef[w, entry * 3] * held[w]
                for d in (1, 2):
                    total = total + coef[w, entry * 3 + d] * held[w + d]
                a, b = total[:, :coeffs], total[:, coeffs:]
                stack += [a, b]
            left = entry * coeffs
            mixed[:, left : left + coeffs] = jnp.concatenate(stack, 0).astype(jnp.bfloat16)
        lhs = mixed[...]
        by_real, by_imag = (
            jnp.dot(lhs, table[part].reshape(depth, coeffs), preferred_element_type=jnp.float32)
            for part in (0, 1)
        )
        for w in range(local):
            top = 2 * w * sources
            mid, low = top + sources, top + 2 * sources
            a = by_real[top:mid] - by_imag[mid:low]
            b = by_real[mid:low] + by_imag[top:mid]
            c = turn[w, 0, :1]
            d = turn[w, 1, :1]
            out[0, f, w, :, :coeffs] = (a * c - b * d).astype(jnp.bfloat16)
            out[0, f, w, :, coeffs:] = (a * d + b * c).astype(jnp.bfloat16)

        @pl.when(f >= 2)
        def _():
            @pl.when(sends & has_low)
            def _():
                send_low(f - 2).wait_send()

            @pl.when(sends & has_high)
            def _():
                send_high(f - 2).wait_send()

            @pl.when(sends)
            def _():
                send_own(f - 2).wait_send()

        @pl.when(sends & has_low)
        def _():
            send_low(f).start()

        @pl.when(sends & has_high)
        def _():
            send_high(f).start()

        @pl.when(sends)
        def _():
            send_own(f).start()

        return carry

    lax.fori_loop(0, fronts, step, 0)

    @pl.when(first & has_low)
    def _():
        for f in range(fronts):
            seed_low(f).wait_send()

    @pl.when(first & has_high)
    def _():
        for f in range(fronts):
            seed_high(f).wait_send()

    @pl.when(sends & has_low)
    def _():
        for f in range(max(fronts - 2, 0), fronts):
            send_low(f).wait_send()

    @pl.when(sends & has_high)
    def _():
        for f in range(max(fronts - 2, 0), fronts):
            send_high(f).wait_send()

    @pl.when(sends)
    def _():
        for f in range(max(fronts - 2, 0), fronts):
            send_own(f).wait_send()


def solution(mesh):
    wins, secs = mesh.shape["win"], mesh.shape["sec"]

    def run(initial, props, screen, links, kinds, counts):
        fronts, local, sources, width = initial.shape
        coeffs = width // 2
        entries = props.shape[1]
        smem = pl.BlockSpec(memory_space=pltpu.SMEM)
        vmem = pl.BlockSpec(memory_space=pltpu.VMEM)
        whole = pl.BlockSpec(memory_space=pl.ANY)
        return pl.pallas_call(
            functools.partial(kernel, wins, secs),
            out_shape=pltpu.VMEM((1, fronts, local, sources, width), jnp.bfloat16),
            in_specs=[smem, smem, smem, vmem, whole, whole],
            out_specs=vmem,
            scratch_shapes=[
                pltpu.VMEM((fronts, local + 2, sources, width), jnp.bfloat16),
                pltpu.VMEM((2, entries, coeffs, coeffs), jnp.bfloat16),
                pltpu.VMEM((2 * local * sources, entries * coeffs), jnp.bfloat16),
                pltpu.SMEM((local, 3 * entries), jnp.float32),
                pltpu.VMEM((local, 2, 8, coeffs), jnp.float32),
                pltpu.SemaphoreType.DMA((2,)),
                pltpu.SemaphoreType.DMA((fronts, 2)),
                pltpu.SemaphoreType.DMA((fronts, 3)),
                pltpu.SemaphoreType.DMA((fronts, 3)),
            ],
            compiler_params=pltpu.CompilerParams(collective_id=0, has_side_effects=True),
            name="beamlets",
        )(links, kinds, counts, screen, initial, props[0])

    placed = (
        P(None, "win", None, None),
        P("sec", None, None, None, None),
        P("sec", "win", None),
        P("sec", "win", None),
        P("sec", "win", None),
        P("sec", "win"),
    )
    return jax.shard_map(
        run,
        mesh=mesh,
        in_specs=placed,
        out_specs=P("sec", None, "win", None, None),
        check_vma=False,
    )
```
